256 devices in a mesh: section: 8 (over x, z_hi), expert: 8 (over z_lo, core), tensor: 4 (over y).
Axes of the slice: x: 4, y: 4, z: 8 (z_hi: 2, z_lo: 4; z = z_hi * 4 + z_lo), core: 2. Of those that a mesh axis runs over, the one named last changes fastest.
Arguments:
- tokens: bfloat16 [512, 6144], P(('section', 'expert'), 'tensor'), may hold values from -6 to 6
- routes: int32 [512, 2], P(('section', 'expert')), may hold values from 0 to 7, all different within a row; in each aligned block of 8 rows (0 to 7, 8 to 15, ...) at most 4 rows name the same one
- router: float32 [6144, 8], replicated, may hold values from -0.18 to 0.18
- gate_proj: bfloat16 [8, 6144, 8192], P('expert', None, ('section', 'tensor')), may hold values from -0.078125 to 0.078125
- up_proj: bfloat16 [8, 6144, 8192], P('expert', None, ('section', 'tensor')), may hold values from -0.078125 to 0.078125
- down_proj: bfloat16 [8, 8192, 6144], P('expert', ('section', 'tensor')), may hold values from -0.125 to 0.125
- grad_out: bfloat16 [512, 6144], P(('section', 'expert'), 'tensor'), may hold values from -6 to 6
Outputs:
- moe_out: bfloat16 [512, 6144], P(('section', 'expert'), 'tensor')
- grad_tokens: bfloat16 [512, 6144], P(('section', 'expert'), 'tensor')
- grad_router: float32 [6144, 8], P('tensor')
The draws below stay inside these ranges and needn't reach their ends.
Inputs may be any that keep to these rules, and one draw needn't show every extreme that they name: `routes`: each token names 2 different experts; in each aligned block of 8 tokens (the tokens of one group) no expert is named by more than 4 tokens, and in some blocks one expert is named by exactly 4.
All inputs are finite; a program needn't handle non-finite values.
Results may differ from the reference program's by a relative error of at most 0.02.
Values may be sent and summed in bfloat16 or wider, within the bound.
No kernel may reach another device: no remote copies, remote signals or barrier semaphores. Data moves between devices by JAX's collectives and lax.ppermute only.
A program may use at most 64 MiB of HBM per device.

```python
import math
import jax
import jax.numpy as jnp
import numpy as np
from jax import lax

D = 6144
FF = 8192
TOP = 2
TOK_DEV = 8
EXPERTS = 8
TOKENS = 512
CAP = 4
FF_DEV = 256
N_SECTION = 8
N_TENSOR = 4


def strengthened(result, rng, source, target, shards_of, factor):
    owner, partner = [(jnp.arange(result.shape[dim]) // (result.shape[dim] // shards_of)).reshape([-1 if axis == dim else 1 for axis in range(result.ndim)]) for dim in (source, target)]
    chosen = jax.random.permutation(rng, shards_of)[partner]
    strong = (owner == chosen) | (owner == (partner + shards_of // 2) % shards_of)
    return jnp.where(strong, factor * result, result)


def steps_of(own_key, extent, cuts, least, high):
    loudness, own = 1.0, jax.random.fold_in(own_key, 6)
    for axis_at, shards_of in cuts:
        draws = jnp.exp(jax.random.uniform(jax.random.fold_in(own, axis_at), (shards_of,), jnp.float32, least / len(cuts), high / len(cuts)))
        loudness = loudness * jnp.repeat(draws, extent[axis_at] // shards_of).reshape([-1 if axis == axis_at else 1 for axis in range(len(extent))])
    return loudness


def shared_out(rng, own, number, rows, amount, top, limit, lean):
    ranking = jax.random.permutation(rng, amount)
    heavy_load, ordinary = shares(amount, rows * top, limit, lean, True), shares(amount, rows * top, limit, lean, False)
    places = jnp.arange(amount)

    def named(sizes, rotation):
        used = int((sizes > 0).sum())
        fixed = max(1, used // 4)
        moved = fixed + (places - fixed + rotation * (used - fixed)) % max(1, amount - fixed)
        return jnp.zeros((amount,), jnp.int32).at[ranking[jnp.where(places < fixed, places, moved)]].set(jnp.asarray(sizes, jnp.int32))

    sizes = jnp.where(number % 4 == 0, named(heavy_load, number // 4), named(ordinary, number - number // 4 - 1))
    mixed = jax.random.permutation(jax.random.fold_in(own, 3), amount)
    giver, sink = mixed[0:amount // 2 * 2:2], mixed[1:amount // 2 * 2:2]
    room = jnp.minimum(sizes[giver] - 1, limit - sizes[sink]) // 2
    room = jnp.where((giver == ranking[0]) | (sink == ranking[0]) | (sizes[sink] == 0), 0, jnp.maximum(room, 0))
    moved = jax.random.randint(jax.random.fold_in(own, 4), (amount // 2,), 0, 1 << 20) % (room + 1)
    sizes = sizes.at[giver].add(-moved).at[sink].add(moved)
    items = jnp.searchsorted(jnp.cumsum(sizes), jnp.arange(rows * top), side="right").astype(jnp.int32)
    listing = items.reshape(top, rows).T
    listing = listing[jax.random.permutation(jax.random.fold_in(own, 1), rows)]
    rotation = jax.random.randint(jax.random.fold_in(own, 2), (rows, 1), 0, top)
    return jnp.take_along_axis(listing, (jnp.arange(top)[None, :] + rotation) % top, axis=1)


def shares(count, total, limit, skew, full):
    loads = [(1 << 20) // math.isqrt(standing ** skew) + 1 for standing in range(1, count + 1)]
    largest = limit if full else min(limit, max(-(-total // count), total * loads[0] // sum(loads)))
    least = 1 if total - largest >= count - 1 else 0
    given, surplus = [largest] + [least] * (count - 1), total - largest - least * (count - 1)
    while surplus > 0:
        movable = [i for i in range(1, count) if given[i] < largest] or [i for i in range(1, count) if given[i] < limit]
        pool, budget = sum([loads[i] for i in movable]), surplus
        for i in movable:
            addition = min(limit - given[i], max(1, budget * loads[i] // pool), surplus)
            given[i] = given[i] + addition
            surplus = surplus - addition
    return np.array(given)


def centred(key, dims, scale, limit, shards=(), kind=jnp.bfloat16):
    level = steps_of(key, dims, shards, -0.22, 0.18) if shards else 1.0
    array = jax.random.normal(key, dims, jnp.float32) * scale * level
    return jnp.minimum(jnp.maximum(array, -limit), limit).astype(kind)


def heavy_noise(stream_key, extent, deviation, most, shards, heavy, kind=jnp.bfloat16):
    array = deviation * jax.random.normal(stream_key, extent, jnp.float32)
    if shards:
        array = array * steps_of(stream_key, extent, shards, -0.22, 0.18)
    return jnp.clip(strengthened(array, jax.random.fold_in(stream_key, 3), *heavy), -most, most).astype(kind)


def setup_inputs(seed: int = 0) -> dict:
    seeds = jax.random.split(jax.random.key(seed), 8)
    tokens = centred(seeds[0], (TOKENS, D), 1.0, 6.0, ((0, 64), (1, 4)))
    routes_keys = jax.random.split(jax.random.fold_in(seeds[1], 1), TOKENS // TOK_DEV)
    routes_turns = jax.random.permutation(jax.random.fold_in(seeds[1], 3), TOKENS // TOK_DEV)
    routes = jax.vmap(lambda own, number: shared_out(jax.random.fold_in(seeds[1], 2), own, number, TOK_DEV, EXPERTS, TOP, CAP, 2))(routes_keys, routes_turns).reshape((TOKENS, TOP))
    router = centred(seeds[2], (D, EXPERTS), 0.03, 0.18, (), jnp.float32)
    gate_proj = centred(seeds[3], (EXPERTS, D, FF), D ** -0.5, 0.078125, ((0, 8), (2, 32)))
    up_proj = centred(seeds[4], (EXPERTS, D, FF), D ** -0.5, 0.078125, ((0, 8), (2, 32)))
    down_proj = heavy_noise(seeds[5], (EXPERTS, FF, D), FF ** -0.5, 0.125, ((0, 8), (1, 32)), (1, 2, 32, 2.75))
    grad_out = centred(seeds[6], (TOKENS, D), 1.0, 6.0, ((0, 64), (1, 4)))
    return dict(tokens=tokens, routes=routes, router=router, gate_proj=gate_proj, up_proj=up_proj, down_proj=down_proj, grad_out=grad_out)


precise = lax.Precision.HIGHEST


def route_table(routes, expert_count, capacity):
    flat_ids = routes.reshape(-1)
    expert_hot = (flat_ids[:, None] == jnp.arange(expert_count, dtype=jnp.int32)[None, :]).astype(jnp.float32)
    earlier = jnp.cumsum(expert_hot, axis=0) - expert_hot
    slot_ids = jnp.sum(earlier * expert_hot, axis=1).astype(jnp.int32)
    slot_hot = (slot_ids[:, None] == jnp.arange(capacity, dtype=jnp.int32)[None, :]).astype(jnp.float32)
    routing = expert_hot.T[:, None, :] * slot_hot.T[None, :, :]
    return routing.reshape(expert_count * capacity, flat_ids.shape[0])


def gate_weights(logits, routes):
    chosen = jnp.take_along_axis(logits, routes, axis=1)
    scores = jax.nn.sigmoid(chosen)
    totals = jnp.sum(scores, axis=1, keepdims=True)
    return scores, scores / totals


def expert_front(rows_x, gate_mat, up_mat):
    pre_gate = jnp.dot(rows_x, gate_mat, preferred_element_type=jnp.float32)
    pre_up = jnp.dot(rows_x, up_mat, preferred_element_type=jnp.float32)
    gate_sig = jax.nn.sigmoid(pre_gate)
    gate_act = pre_gate * gate_sig
    hidden = (gate_act * pre_up).astype(jnp.bfloat16)
    return pre_gate, pre_up, gate_sig, gate_act, hidden


def expert_grads(grad_hidden, pre_gate, pre_up, gate_sig, gate_act):
    grad_gate = (grad_hidden * pre_up * gate_sig * (1.0 + pre_gate * (1.0 - gate_sig))).astype(jnp.bfloat16)
    grad_up = (grad_hidden * gate_act).astype(jnp.bfloat16)
    return grad_gate, grad_up


def router_grads(grad_weight, scores, routes, expert_count):
    totals = scores[:, 0] + scores[:, 1]
    first = (grad_weight[:, 0] - grad_weight[:, 1]) * scores[:, 1] / (totals * totals)
    second = (grad_weight[:, 1] - grad_weight[:, 0]) * scores[:, 0] / (totals * totals)
    grad_scores = jnp.stack([first, second], axis=1)
    grad_chosen = grad_scores * scores * (1.0 - scores)
    expert_hot = (routes[:, :, None] == jnp.arange(expert_count, dtype=jnp.int32)[None, None, :]).astype(jnp.float32)
    return jnp.sum(expert_hot * grad_chosen[:, :, None], axis=1)


def rounded_term(value):
    narrow = lax.optimization_barrier(value.astype(jnp.bfloat16))
    return narrow.astype(jnp.float32)


def reference(tokens, routes, router, gate_proj, up_proj, down_proj, grad_out):
    groups = TOKENS // TOK_DEV
    shard_count = N_SECTION * N_TENSOR
    wide_tokens = tokens.astype(jnp.float32)
    logits = jnp.dot(wide_tokens, router, precision=precise)
    scores, weight = gate_weights(logits, routes)
    routing = jax.vmap(lambda part_ids: route_table(part_ids, EXPERTS, CAP))(routes.reshape(groups, TOK_DEV, TOP))
    tokens_rep = jnp.repeat(wide_tokens.reshape(groups, TOK_DEV, D), TOP, axis=1)
    grads_rep = jnp.repeat(grad_out.astype(jnp.float32).reshape(groups, TOK_DEV, D), TOP, axis=1) * weight.reshape(groups, TOK_DEV * TOP, 1)
    x_sent = jnp.einsum("gkr,grd->gkd", routing, tokens_rep, precision=precise).astype(jnp.bfloat16)
    dy_sent = jnp.einsum("gkr,grd->gkd", routing, grads_rep, precision=precise).astype(jnp.bfloat16)

    def by_expert(buffer):
        return buffer.reshape(groups, EXPERTS, CAP, D).transpose(1, 0, 2, 3).reshape(EXPERTS, groups * CAP, D)

    def split_columns(matrix):
        return matrix.reshape(matrix.shape[0], shard_count, FF_DEV).transpose(1, 0, 2)

    def expert_pass(members):
        rows_x, rows_dy, gate_mat, up_mat, down_mat = members
        pre_gate, pre_up, gate_sig, gate_act, hidden = expert_front(rows_x, gate_mat, up_mat)
        grad_hidden = jnp.dot(rows_dy, down_mat.T, preferred_element_type=jnp.float32)
        grad_gate, grad_up = expert_grads(grad_hidden, pre_gate, pre_up, gate_sig, gate_act)
        pieces = (split_columns(hidden), split_columns(grad_gate), split_columns(grad_up),
                  split_columns(gate_mat), split_columns(up_mat), down_mat.reshape(shard_count, FF_DEV, D))

        def add_block(carry, piece):
            hid_part, gg_part, gu_part, gate_part, up_part, down_part = piece
            out_term = jnp.dot(hid_part, down_part, preferred_element_type=jnp.float32)
            grad_term = jnp.dot(gg_part, gate_part.T, preferred_element_type=jnp.float32) + jnp.dot(gu_part, up_part.T, preferred_element_type=jnp.float32)
            return (carry[0] + rounded_term(out_term), carry[1] + rounded_term(grad_term)), None

        start = (jnp.zeros((rows_x.shape[0], D), jnp.float32), jnp.zeros((rows_x.shape[0], D), jnp.float32))
        (expert_out, expert_grad), _ = lax.scan(add_block, start, pieces)
        return expert_out, expert_grad

    outs_all, grads_all = lax.map(expert_pass, (by_expert(x_sent), by_expert(dy_sent), gate_proj, up_proj, down_proj))

    def to_groups(values):
        return values.reshape(EXPERTS, groups, CAP, D).transpose(1, 0, 2, 3).reshape(groups, EXPERTS * CAP, D)

    out_route = jnp.einsum("gkr,gkd->grd", routing, to_groups(outs_all), precision=precise).reshape(TOKENS, TOP, D)
    grad_route = jnp.einsum("gkr,gkd->grd", routing, to_groups(grads_all), precision=precise).reshape(TOKENS, TOP, D)
    moe_out = jnp.sum(weight[:, :, None] * out_route, axis=1).astype(jnp.bfloat16)
    grad_weight = jnp.sum(grad_out.astype(jnp.float32)[:, None, :] * out_route, axis=2)
    grad_logits = router_grads(grad_weight, scores, routes, EXPERTS)
    grad_tokens = (jnp.sum(grad_route, axis=1) + jnp.dot(grad_logits, router.T, precision=precise)).astype(jnp.bfloat16)
    grad_router = jnp.dot(wide_tokens.T, grad_logits, precision=precise)
    return moe_out, grad_tokens, grad_router
```

```python
import jax
import jax.numpy as jnp
from jax import lax
from jax.experimental import pallas as pl
from jax.experimental.pallas import tpu as pltpu
from jax.sharding import Mesh
from jax.sharding import PartitionSpec as P

F32 = jnp.float32
BF16 = jnp.bfloat16
ZAX = ("zh", "zl", "c")
EXP = ("zl", "c")
ALL = ("x", "zh", "zl", "c")
RING = 4
OFFS = (0, -1, 1, 2)
N_EXP = 8
CAP = 4
SLOTS = N_EXP * CAP
LANES = 128


def dot(a, b):
    return jnp.dot(a, b, preferred_element_type=F32)


def dot_t(a, b):
    return lax.dot_general(a, b, (((1,), (1,)), ((), ())), preferred_element_type=F32)


def shift(a, axis, n):
    return lax.ppermute(a, axis, [(i, (i + n) % RING) for i in range(RING)])


def sds(shape, dtype):
    return jax.ShapeDtypeStruct(shape, dtype)


VMEM = pl.BlockSpec(memory_space=pltpu.VMEM)
SMEM = pl.BlockSpec(memory_space=pltpu.SMEM)


def local(body, outs, *args, smem=0, limit=16, alias=None):
    return pl.pallas_call(
        body,
        out_shape=outs,
        in_specs=[SMEM] * smem + [VMEM] * (len(args) - smem),
        out_specs=jax.tree.map(lambda _: VMEM, outs),
        input_output_aliases=alias or {},
        compiler_params=pltpu.CompilerParams(vmem_limit_bytes=limit << 20),
    )(*args)


def ring_gather(a, axis):
    half = a.shape[0] // 2
    left = shift(a, axis, 1)
    right = shift(a, axis, -1)
    return a, left, right, shift(left[:half], axis, 1), shift(right[half:], axis, -1)


def add_body(right, up, left, down, right_out, left_out):
    half = up.shape[0]
    right_out[:half] = (right[:half].astype(F32) + up[...].astype(F32)).astype(BF16)
    right_out[half:] = right[half:]
    left_out[:half] = left[:half]
    left_out[half:] = (left[half:].astype(F32) + down[...].astype(F32)).astype(BF16)


def ring_reduce(own, left, right, far_t, far_b, axis):
    up = shift(far_t, axis, 1)
    down = shift(far_b, axis, -1)
    like = sds(right.shape, BF16)
    right, left = local(add_body, (like, like), right, up, left, down)
    return own, shift(right, axis, 1), shift(left, axis, -1)


def split3(a):
    hi = a.astype(BF16)
    rest = a - hi.astype(F32)
    mid = rest.astype(BF16)
    low = (rest - mid.astype(F32)).astype(BF16)
    return hi, mid, low


def rows_body(own, left, right, far, rows_out, meta_out):
    n, width = own.shape
    for i, r in enumerate((own, left, right, far)):
        rows_out[i * n : (i + 1) * n] = r[:, : width - LANES]
        meta_out[i * n : (i + 1) * n] = r[:, width - LANES :]


def lanes_body(parts, out):
    n, rows, width = parts.shape
    for i in range(n):
        out[:, i * width : (i + 1) * width] = parts[i]


def front_body(
    at, x0, x1, x2, x3t, x3b, d0, d1, d2, d3t, d3b, meta, gate, up, down, router,
    hidden_out, gg_out, gu_out, tl_out, gate_out,
):
    y_at, e_at = at[0], at[1]
    quarter = x0.shape[1]
    pre_gate = pre_up = logits3 = None
    for i, off in enumerate(OFFS):
        q = pl.multiple_of(((y_at + (off + RING)) % RING) * quarter, quarter)
        a = (x0[...], x1[...], x2[...])[i] if i < 3 else jnp.concatenate([x3t[...], x3b[...]], 0)
        rows = pl.ds(q, quarter)
        g, u, r = dot(a, gate[rows]), dot(a, up[rows]), dot(a, router[rows])
        pre_gate = g if i == 0 else pre_gate + g
        pre_up = u if i == 0 else pre_up + u
        logits3 = r if i == 0 else logits3 + r
    raw = None
    for k in range(RING):
        cols = slice(k * quarter, (k + 1) * quarter)
        a = jnp.concatenate([d0[:, cols], d1[:, cols], d2[:, cols], d3t[:, cols], d3b[:, cols]], 0)
        g = dot_t(a, down[:, cols])
        raw = g if k == 0 else raw + g
    lane = lax.broadcasted_iota(jnp.int32, logits3.shape, 1)
    inside = lane < 3 * N_EXP
    expert = lane % N_EXP
    code = meta[...].astype(F32).astype(jnp.int32)
    other = code // CAP
    hot_own = (expert == e_at) & inside
    hot_other = (expert == other) & inside
    logit_own = jnp.sum(jnp.where(hot_own, logits3, 0.0), 1, keepdims=True)
    logit_other = jnp.sum(jnp.where(hot_other, logits3, 0.0), 1, keepdims=True)
    score_own = jax.nn.sigmoid(logit_own)
    score_other = jax.nn.sigmoid(logit_other)
    total = score_own + score_other
    weight = score_own / total
    both = score_own * score_other / (total * total)
    c_own = both * (1.0 - score_own)
    c_other = both * (1.0 - score_other)
    gate_sig = jax.nn.sigmoid(pre_gate)
    gate_act = pre_gate * gate_sig
    hidden = gate_act * pre_up
    grad_weight = jnp.sum(hidden * raw, 1, keepdims=True)
    hidden_out[...] = (weight * hidden).astype(BF16)
    grad_hidden = weight * raw
    gg_out[...] = (
        grad_hidden * pre_up * gate_sig * (1.0 + pre_gate * (1.0 - gate_sig))
    ).astype(BF16)
    gu_out[...] = (grad_hidden * gate_act).astype(BF16)
    wide = lane < 4 * N_EXP
    to_logits = jnp.where((expert == e_at) & wide, grad_weight * c_own, 0.0) - jnp.where(
        (expert == other) & wide, grad_weight * c_other, 0.0
    )
    high = to_logits.astype(BF16).astype(F32)
    tl_out[...] = jnp.where((lane // N_EXP) % 2 == 0, high, to_logits - high).astype(BF16)
    gate_out[...] = jnp.where(lane == 0, grad_weight, jnp.where(lane == 1, c_own, 0.0))


def back_body(
    at, hidden, gg, gu, tl, gate, up, down, router,
    m0, m1, m2, m3t, m3b, g0, g1, g2, g3t, g3b,
):
    y_at = at[0]
    quarter = m0.shape[1]
    own = g0.shape[0]
    for i in (3, 1, 2, 0):
        q = pl.multiple_of(((y_at + (OFFS[i] + RING)) % RING) * quarter, quarter)
        v = dot(hidden[...], down[:, pl.ds(q, quarter)]).astype(BF16)
        if i == 3:
            half = m3t.shape[0]
            m3t[...] = v[:half]
            m3b[...] = v[half:]
        else:
            (m0, m1, m2)[i][...] = v
    step = 512
    for k in range(RING * quarter // step):
        at_k = slice(k * step, (k + 1) * step)
        v = dot_t(gg[...], gate[at_k]) + dot_t(gu[...], up[at_k]) + dot_t(tl[...], router[at_k])
        v = v.astype(BF16)
        g0[:, at_k] = v[:own]
        g1[:, at_k] = v[own : 2 * own]
        g2[:, at_k] = v[2 * own : 3 * own]
        g3t[:, at_k] = v[3 * own : 3 * own + own // 2]
        g3b[:, at_k] = v[3 * own + own // 2 :]


def sum_rows_body(a, b, c, o0, o1, o2, o3):
    n = o0.shape[0]
    for i, o in enumerate((o0, o1, o2, o3)):
        s = slice(i * n, (i + 1) * n)
        o[...] = (a[s].astype(F32) + b[s].astype(F32) + c[s].astype(F32)).astype(BF16)


def sum_lanes_body(a, b, c, out):
    n, rows, width = out.shape
    for i in range(n):
        s = slice(i * width, (i + 1) * width)
        out[i] = (a[:, s].astype(F32) + b[:, s].astype(F32) + c[:, s].astype(F32)).astype(BF16)


def on_device(tokens, routes, router, gate_proj, up_proj, down_proj, grad_out):
    rows, quarter = tokens.shape
    y_at = lax.axis_index("y")
    x_at = lax.axis_index("x")
    e_at = lax.axis_index(EXP)
    at = jnp.stack([y_at, e_at]).astype(jnp.int32)
    gate, up, down = gate_proj[0], up_proj[0], down_proj[0]
    width = RING * quarter

    flat = routes.reshape(-1)
    ids = jnp.arange(flat.shape[0], dtype=jnp.int32)
    same = (flat[:, None] == flat[None, :]) & (ids[None, :] < ids[:, None])
    slot = jnp.sum(same.astype(jnp.int32), axis=1)
    code = (flat * CAP + slot).reshape(rows, 2)
    lanes = jnp.arange(SLOTS, dtype=jnp.int32)
    hot = (code[:, :, None] == lanes[None, None, :]).astype(F32)
    pick_b = jnp.sum(hot, axis=1).astype(BF16)
    meta = jnp.sum(hot * code[:, ::-1, None].astype(F32), axis=(0, 1))

    def pack(a):
        return lax.dot_general(
            pick_b, a, (((0,), (0,)), ((), ())), preferred_element_type=F32
        ).astype(BF16)

    packed = jnp.concatenate(
        [pack(tokens), jnp.broadcast_to(meta[:, None], (SLOTS, LANES)).astype(BF16), pack(grad_out)], 1
    ).reshape(N_EXP, CAP, -1)
    got = lax.all_to_all(jnp.concatenate([packed, packed], 0), ZAX, 0, 0, tiled=True)
    got = got.reshape(2 * SLOTS, -1)
    got_x, got_dy = got[:, : quarter + LANES], got[:, quarter + LANES :]
    n_own = got.shape[0]
    n_rows = RING * n_own

    got_dy = lax.all_to_all(
        jnp.broadcast_to(got_dy, (RING, n_own, quarter)), "y", 0, 0, tiled=True
    )
    pieces = [got_x] + [shift(got_x, "x", n) for n in (1, -1, 2)]
    row_x, meta_all = local(
        rows_body, (sds((n_rows, quarter), BF16), sds((n_rows, LANES), BF16)), *pieces
    )
    row_dy = local(lanes_body, sds((n_own, width), BF16), got_dy)
    full_x = ring_gather(row_x, "y")
    full_dy = ring_gather(row_dy, "x")

    parts = split3(router)
    pad = jnp.zeros((width, LANES - 3 * N_EXP), BF16)
    router_in = jnp.concatenate([*parts, pad], 1)
    pad = jnp.zeros((width, LANES - 4 * N_EXP), BF16)
    router_out = jnp.concatenate([parts[0], parts[0], parts[1], parts[1], pad], 1)

    n_ff = gate.shape[1]
    act = sds((n_rows, n_ff), BF16)
    hidden, grad_gate, grad_up, to_logits, gates = local(
        front_body,
        (act, act, act, sds((n_rows, LANES), BF16), sds((n_rows, LANES), F32)),
        at, *full_x, *full_dy, meta_all, gate, up, down, router_in, smem=1,
    )
    far = sds((n_rows // 2, quarter), BF16)
    near = sds((n_rows, quarter), BF16)
    g_far = sds((n_own // 2, width), BF16)
    g_near = sds((n_own, width), BF16)
    parts = local(
        back_body,
        (near, near, near, far, far, g_near, g_near, g_near, g_far, g_far),
        at, hidden, grad_gate, grad_up, to_logits, gate, up, down, router_out, smem=1,
    )

    grad_weight, c_own = gates[:, 0], gates[:, 1:2]
    spots = (x_at + jnp.array(OFFS, dtype=jnp.int32) + RING) % RING
    place = (spots[:, None] == jnp.arange(RING, dtype=jnp.int32)[None, :]).astype(F32)
    gw_abs = jnp.sum(place[:, :, None] * grad_weight.reshape(RING, 1, n_own), 0).reshape(1, n_rows)
    n_shards = 2 * RING * RING
    gw_all = lax.all_to_all(
        jnp.broadcast_to(gw_abs, (n_shards, n_rows)).reshape(n_shards, 2, n_rows // 2),
        ("x", "zh", "y"), 0, 0, tiled=True,
    )
    gw_sum = jnp.sum(gw_all, 0)[None]
    gw_exp = lax.all_to_all(
        jnp.broadcast_to(gw_sum, (N_EXP, 2, n_rows // 2)), EXP, 0, 0, tiled=True
    ).reshape(N_EXP, n_rows // CAP, CAP)
    gw_group = gw_exp.transpose(1, 0, 2).reshape(RING, n_own // CAP, SLOTS)
    gw_group = jnp.sum(place[:, :, None, None] * gw_group[None], 1).reshape(n_rows // CAP, 1, SLOTS)
    gw_group = jnp.broadcast_to(gw_group, (n_rows // CAP, CAP, SLOTS)).reshape(n_rows, SLOTS)
    own_code = e_at * CAP + jnp.arange(n_rows, dtype=jnp.int32)[:, None] % CAP
    meta_int = meta_all[:, :1].astype(jnp.int32)
    pair_hot = (lanes[None, :] == own_code).astype(F32) - (lanes[None, :] == meta_int).astype(F32)
    grad_logit = c_own * jnp.sum(gw_group * pair_hot, 1, keepdims=True)
    gl_parts = jnp.concatenate(split3(grad_logit), 1)
    column = lax.dot_general(
        gl_parts, row_x, (((0,), (0,)), ((), ())), preferred_element_type=F32
    )
    column = jnp.sum(column, 0).reshape(1, quarter // LANES, LANES)
    columns = lax.all_to_all(
        jnp.broadcast_to(column, (N_EXP, quarter // LANES, LANES)), EXP, 0, 0, tiled=True
    )
    grad_router = columns.reshape(N_EXP, quarter).T

    out_terms = ring_reduce(*parts[:5], "y")
    grad_terms = ring_reduce(*parts[5:], "x")
    piece = sds((n_own, quarter), BF16)
    out_x = local(sum_rows_body, (piece,) * RING, *out_terms)
    grad_y = local(sum_lanes_body, sds((RING, n_own, quarter), BF16), *grad_terms)
    out_got = [out_x[0]] + [shift(out_x[i], "x", OFFS[i]) for i in (1, 2, 3)]
    out_own = sum(a.astype(F32) for a in out_got).astype(BF16)
    grad_got = lax.all_to_all(grad_y, "y", 0, 0, tiled=True)
    grad_own = jnp.sum(grad_got.astype(F32), 0).astype(BF16)

    final = jnp.concatenate([out_own, grad_own], 1).reshape(2 * N_EXP, CAP, -1)
    final = lax.all_to_all(final, ZAX, 0, 0, tiled=True).reshape(2 * SLOTS, -1)
    both = dot(jnp.concatenate([pick_b, pick_b], 1), final).astype(BF16)
    return (both[:, :quarter], both[:, quarter:], grad_router)


def solution(mesh):
    fine = Mesh(mesh.devices.reshape(4, 2, 4, 2, 4), ("x", "zh", "zl", "c", "y"))
    return jax.shard_map(
        on_device,
        mesh=fine,
        in_specs=(
            P(ALL, "y"),
            P(ALL, None),
            P(),
            P(EXP, None, ("x", "zh", "y")),
            P(EXP, None, ("x", "zh", "y")),
            P(EXP, ("x", "zh", "y"), None),
            P(ALL, "y"),
        ),
        out_specs=(P(ALL, "y"), P(ALL, "y"), P("y", None)),
        check_vma=False,
    )
```

```python
import jax
import jax.numpy as jnp
from jax import lax
from jax.experimental import pallas as pl
from jax.experimental.pallas import tpu as pltpu
from jax.sharding import Mesh
from jax.sharding import PartitionSpec as P

F32 = jnp.float32
BF16 = jnp.bfloat16
ZAX = ("zh", "zl", "c")
EXP = ("zl", "c")
ALL = ("x", "zh", "zl", "c")
RING = 4
OFFS = (0, -1, 1, 2)
N_EXP = 8
CAP = 4
SLOTS = N_EXP * CAP
LANES = 128


def dot(a, b):
    return jnp.dot(a, b, preferred_element_type=F32)


def dot_t(a, b):
    return lax.dot_general(a, b, (((1,), (1,)), ((), ())), preferred_element_type=F32)


def shift(a, axis, n):
    return lax.ppermute(a, axis, [(i, (i + n) % RING) for i in range(RING)])


def sds(shape, dtype):
    return jax.ShapeDtypeStruct(shape, dtype)


VMEM = pl.BlockSpec(memory_space=pltpu.VMEM)
SMEM = pl.BlockSpec(memory_space=pltpu.SMEM)
ANY = pl.BlockSpec(memory_space=pl.ANY)


def kernel(body, outs, *args, specs, out_specs=None, scratch=(), limit=16):
    return pl.pallas_call(
        body,
        out_shape=outs,
        in_specs=list(specs),
        out_specs=out_specs or jax.tree.map(lambda _: VMEM, outs),
        scratch_shapes=list(scratch),
        compiler_params=pltpu.CompilerParams(vmem_limit_bytes=limit << 20),
    )(*args)


def spot(at, off):
    return (at + (off + RING)) % RING


def rows_body(own, left, right, far, top_out, bot_out, meta_out):
    n, width = own.shape
    for i, r in enumerate((own, left, right, far)):
        s = slice((i % 2) * n, (i % 2 + 1) * n)
        (top_out, bot_out)[i // 2][s] = r[:, : width - LANES]
        meta_out[i * n : (i + 1) * n] = r[:, width - LANES :]


def expert_body(
    at, x0t, x0b, x1t, x1b, x2t, x2b, x3t, x3b, dys, meta, gate, up, down, router,
    m0, m1, m2, m3t, m3b, g0, g1, g2, g3t, g3b, gw_out, gates_out,
    xb, db, gb, ub, wb, mb, rp, hb, ggb, gub, tlb, mo, go, sx, sd, sm, sg, su, sw, so,
):
    x_at, y_at, e_at = at[0], at[1], at[2]
    n = dys.shape[1]
    quarter = dys.shape[2]
    n_rows = RING * n
    half = n_rows // 2
    copies_x, copies_d, copies_m, copies_g, copies_u, copies_w = [], [], [], [], [], []

    def copy(src, dst, sem):
        c = pltpu.make_async_copy(src, dst, sem)
        c.start()
        return c

    def cols(i):
        return slice(i * quarter, (i + 1) * quarter)

    def row_at(i):
        return pl.ds(pl.multiple_of(spot(x_at, OFFS[i]) * n, n), n)

    for i in range(RING):
        pair = ((x0t, x0b), (x1t, x1b), (x2t, x2b), (x3t, x3b))[i]
        q = pl.ds(pl.multiple_of(spot(y_at, OFFS[i]) * quarter, quarter), quarter)
        for r in range(RING):
            src = pair[r // 2].at[(r % 2) * n : (r % 2 + 1) * n]
            copies_x.append(copy(src, xb.at[i, row_at(r), :], sx.at[i * RING + r]))
        copies_g.append(copy(gate.at[q], gb.at[i], sg.at[i]))
        copies_u.append(copy(up.at[q], ub.at[i], su.at[i]))
    for r in range(RING):
        copies_m.append(copy(meta.at[r * n : (r + 1) * n], mb.at[row_at(r), :], sm.at[r]))
    for i in range(RING):
        q = pl.ds(pl.multiple_of(spot(y_at, OFFS[i]) * quarter, quarter), quarter)
        for r in range(RING):
            src = dys.at[r * RING + spot(y_at, OFFS[i])]
            copies_d.append(copy(src, db.at[i, r * n : (r + 1) * n], sd.at[i * RING + r]))
        copies_w.append(copy(down.at[:, q], wb.at[i], sw.at[i]))

    for i in range(RING):
        q = pl.ds(pl.multiple_of(spot(y_at, OFFS[i]) * quarter, quarter), quarter)
        r0 = router[:, q]
        r1 = r0 - r0.astype(BF16).astype(F32)
        r2 = r1 - r1.astype(BF16).astype(F32)
        rp[i] = jnp.concatenate([r0, r1, r2, jnp.zeros_like(r0)], 0).astype(BF16)

    pre_gate = pre_up = logits3 = raw = None
    for i in range(RING):
        for r in range(RING):
            copies_x[i * RING + r].wait()
        copies_g[i].wait()
        copies_u[i].wait()
        a = xb[i]
        g, u, l = dot(a, gb[i]), dot(a, ub[i]), dot_t(a, rp[i])
        pre_gate = g if i == 0 else pre_gate + g
        pre_up = u if i == 0 else pre_up + u
        logits3 = l if i == 0 else logits3 + l
    for i in range(RING):
        for r in range(RING):
            copies_d[i * RING + r].wait()
        copies_w[i].wait()
        g = dot_t(db[i], wb[i])
        raw = g if i == 0 else raw + g
    for c in copies_m:
        c.wait()

    lane = lax.broadcasted_iota(jnp.int32, logits3.shape, 1)
    expert = lane % N_EXP
    code = mb[:, :1].astype(F32).astype(jnp.int32)
    other = code // CAP
    hot_own = expert == e_at
    hot_other = expert == other
    score_own = jax.nn.sigmoid(jnp.sum(jnp.where(hot_own, logits3, 0.0), 1, keepdims=True))
    score_other = jax.nn.sigmoid(jnp.sum(jnp.where(hot_other, logits3, 0.0), 1, keepdims=True))
    total = score_own + score_other
    weight = score_own / total
    both = score_own * score_other / (total * total)
    c_own = both * (1.0 - score_own)
    c_other = both * (1.0 - score_other)
    gate_sig = jax.nn.sigmoid(pre_gate)
    gate_act = pre_gate * gate_sig
    hidden = gate_act * pre_up
    product = hidden * raw
    grad_weight = jnp.sum(product, 1, keepdims=True)
    hb[...] = (weight * hidden).astype(BF16)
    grad_hidden = weight * raw
    ggb[...] = (
        grad_hidden * pre_up * gate_sig * (1.0 + pre_gate * (1.0 - gate_sig))
    ).astype(BF16)
    gub[...] = (grad_hidden * gate_act).astype(BF16)
    to_logits = jnp.where(hot_own, grad_weight * c_own, 0.0) - jnp.where(
        hot_other, grad_weight * c_other, 0.0
    )
    high = to_logits.astype(BF16).astype(F32)
    tlb[...] = jnp.where(lane < 2 * N_EXP, high, to_logits - high).astype(BF16)
    wide = lax.broadcasted_iota(jnp.int32, gates_out.shape, 1)
    gates_out[...] = jnp.where(wide == 0, c_own, code.astype(F32))
    ones = jnp.ones((8, product.shape[1]), F32)
    sums = lax.dot_general(
        ones, product, (((1,), (1,)), ((), ())),
        preferred_element_type=F32, precision=lax.Precision.HIGHEST,
    )
    for k in range(gw_out.shape[0] // 8):
        gw_out[k * 8 : (k + 1) * 8] = sums

    outs = []

    def send(src, dst):
        outs.append(copy(src, dst, so.at[len(outs)]))

    for i in (3, 1, 2, 0):
        mo[i] = dot(hb[...], wb[i]).astype(BF16)
        if i == 3:
            send(mo.at[i, :half], m3t)
            send(mo.at[i, half:], m3b)
        else:
            send(mo.at[i], (m0, m1, m2)[i])
    for i in range(RING):
        r4 = jnp.concatenate([rp[i][: 2 * N_EXP], rp[i][: 2 * N_EXP]], 0)
        v = dot_t(ggb[...], gb[i]) + dot_t(gub[...], ub[i]) + dot(tlb[...], r4)
        go[i] = v.astype(BF16)
        q = pl.ds(pl.multiple_of(spot(y_at, OFFS[i]) * quarter, quarter), quarter)
        for j, dst in ((1, g1), (2, g2), (0, g0)):
            send(go.at[i, row_at(j), :], dst.at[:, q])
        start = pl.multiple_of(spot(x_at, 2) * n, n)
        send(go.at[i, pl.ds(start, n // 2), :], g3t.at[:, q])
        send(go.at[i, pl.ds(pl.multiple_of(start + n // 2, n // 2), n // 2), :], g3b.at[:, q])
    for c in outs:
        c.wait()


def exchange_body(gw_all, out):
    out[...] = jnp.broadcast_to(jnp.sum(gw_all[...], 0, keepdims=True), out.shape)


def column_body(at, gw, gates, top, bot, out, gl):
    x_at, zh_at, e_at = at[0], at[3], at[2]
    n_rows = gates.shape[0]
    n = n_rows // RING
    n_half = top.shape[1] // 2
    row = lax.broadcasted_iota(jnp.int32, (n_rows, n_rows), 0)
    col = lax.broadcasted_iota(jnp.int32, (n_rows, n_rows), 1)
    code = gates[:, 1:2].astype(jnp.int32)
    mate = (row // CAP) * CAP + code % CAP

    def fetch(mask):
        return lax.dot_general(
            mask.astype(F32), gw[...], (((1,), (1,)), ((), ())),
            preferred_element_type=F32, precision=lax.Precision.HIGHEST,
        )

    lane = lax.broadcasted_iota(jnp.int32, (n_rows, N_EXP), 1)
    diff = jnp.where(lane == e_at, fetch(row == col), 0.0) - jnp.where(
        lane == code // CAP, fetch(mate == col), 0.0
    )
    gl[...] = jnp.broadcast_to(gates[:, :1] * jnp.sum(diff, 1, keepdims=True), gl.shape)
    feat = pl.ds(pl.multiple_of(zh_at * n_half, n_half), n_half)
    acc = None
    for i in range(RING):
        a = (top, bot)[i // 2][(i % 2) * n : (i % 2 + 1) * n, feat].astype(F32)
        g = gl[pl.ds(pl.multiple_of(spot(x_at, OFFS[i]) * n, n), n), :1]
        s = jnp.sum(a * g, 0, keepdims=True)
        acc = s if i == 0 else acc + s
    q = n_half // 2
    high = acc.astype(BF16).astype(F32)
    low = acc - high
    four = jnp.concatenate([high[:, :q], high[:, q:], low[:, :q], low[:, q:]], 0)
    block = jnp.concatenate([four, four], 0)
    for k in range(out.shape[0] // 16):
        out[k * 16 : (k + 1) * 16] = jnp.concatenate([block, block], 0).astype(BF16)


def add_body(right, up, left, down, right_out, left_out):
    right_out[...] = (right[...].astype(F32) + up[...].astype(F32)).astype(BF16)
    left_out[...] = (left[...].astype(F32) + down[...].astype(F32)).astype(BF16)


def ring_reduce(own, left, right, far_t, far_b, axis):
    up = shift(far_t, axis, 1)
    down = shift(far_b, axis, -1)
    half, width = far_t.shape
    steps = 4
    top = pl.BlockSpec((half, width // steps), lambda j: (0, j))
    bottom = pl.BlockSpec((half, width // steps), lambda j: (1, j))
    like = sds(right.shape, BF16)
    right, left = pl.pallas_call(
        add_body,
        grid=(steps,),
        out_shape=(like, like),
        in_specs=[top, top, bottom, top],
        out_specs=(top, bottom),
        input_output_aliases={0: 0, 2: 1},
        compiler_params=pltpu.CompilerParams(vmem_limit_bytes=16 << 20),
    )(right, up, left, down)
    return own, shift(right, axis, 1), shift(left, axis, -1)


def sum_rows_body(at, a, b, c, o0, o1, o2, o3):
    n = o0.shape[0]
    for i, o in enumerate((o0, o1, o2, o3)):
        s = pl.ds(pl.multiple_of(spot(at[0], OFFS[i]) * n, n), n)
        o[...] = (a[s].astype(F32) + b[s].astype(F32) + c[s].astype(F32)).astype(BF16)


def sum_rows(at, a, b, c):
    rows, width = a.shape
    steps = 4
    full = pl.BlockSpec((rows, width // steps), lambda j: (0, j))
    part = pl.BlockSpec((rows // RING, width // steps), lambda j: (0, j))
    return pl.pallas_call(
        sum_rows_body,
        grid=(steps,),
        out_shape=(sds((rows // RING, width), BF16),) * RING,
        in_specs=[SMEM] + [full] * 3,
        out_specs=(part,) * RING,
        compiler_params=pltpu.CompilerParams(vmem_limit_bytes=16 << 20),
    )(at, a, b, c)


def sum_lanes_body(a, b, c, out):
    out[0] = (a[...].astype(F32) + b[...].astype(F32) + c[...].astype(F32)).astype(BF16)


def sum_lanes(a, b, c):
    rows, width = a.shape
    part = pl.BlockSpec((rows, width // RING), lambda j: (0, j))
    return pl.pallas_call(
        sum_lanes_body,
        grid=(RING,),
        out_shape=sds((RING, rows, width // RING), BF16),
        in_specs=[part] * 3,
        out_specs=pl.BlockSpec((1, rows, width // RING), lambda j: (j, 0, 0)),
        compiler_params=pltpu.CompilerParams(vmem_limit_bytes=16 << 20),
    )(a, b, c)


def last_body(a0, a1, a2, a3, g, column, out):
    width = a0.shape[1]
    total = a0[...].astype(F32) + a1[...].astype(F32) + (a2[...].astype(F32) + a3[...].astype(F32))
    out[:, :width] = total.astype(BF16)
    total = g[0].astype(F32) + g[1].astype(F32) + (g[2].astype(F32) + g[3].astype(F32))
    out[:, width : 2 * width] = total.astype(BF16)
    out[:, 2 * width :] = column[...]


def combine_body(pick, got, moe_out, gt_out, gr_out):
    width = moe_out.shape[1]
    two = pick[...]
    moe_out[...] = dot(two, got[:, :width]).astype(BF16)
    gt_out[...] = dot(two, got[:, width : 2 * width]).astype(BF16)
    tail = got[:, 2 * width :]
    q = tail.shape[1]
    n_got = got.shape[0]
    e = lax.broadcasted_iota(jnp.int32, (N_EXP, n_got), 0)
    r = lax.broadcasted_iota(jnp.int32, (N_EXP, n_got), 1)
    for zh in range(2):
        for c in range(2):
            base = (zh * N_EXP + e) * CAP + c
            high, low = ((r == base + k).astype(F32).astype(BF16) for k in (0, 2))
            parts = dot(high, tail) + dot(low, tail)
            gr_out[:, (zh * 2 + c) * q : (zh * 2 + c + 1) * q] = parts


def on_device(tokens, routes, router, gate_proj, up_proj, down_proj, grad_out):
    rows, quarter = tokens.shape
    at = jnp.stack(
        [lax.axis_index("x"), lax.axis_index("y"), lax.axis_index(EXP), lax.axis_index("zh")]
    ).astype(jnp.int32)
    gate, up, down = gate_proj[0], up_proj[0], down_proj[0]
    width = RING * quarter
    n_ff = gate.shape[1]

    flat = routes.reshape(-1)
    ids = jnp.arange(flat.shape[0], dtype=jnp.int32)
    same = (flat[:, None] == flat[None, :]) & (ids[None, :] < ids[:, None])
    slot = jnp.sum(same.astype(jnp.int32), axis=1)
    code = (flat * CAP + slot).reshape(rows, 2)
    lanes = jnp.arange(SLOTS, dtype=jnp.int32)
    hot = (code[:, :, None] == lanes[None, None, :]).astype(F32)
    pick_b = jnp.sum(hot, axis=1).astype(BF16)
    meta = jnp.sum(hot * code[:, ::-1, None].astype(F32), axis=(0, 1))

    def pack(a):
        return lax.dot_general(
            pick_b, a, (((0,), (0,)), ((), ())), preferred_element_type=F32
        ).astype(BF16)

    def to_owner(a):
        a = a.reshape(N_EXP, CAP, -1)
        a = lax.all_to_all(jnp.concatenate([a, a], 0), ZAX, 0, 0, tiled=True)
        return a.reshape(2 * SLOTS, -1)

    meta = jnp.broadcast_to(meta[:, None], (SLOTS, LANES)).astype(BF16)
    got_x = to_owner(jnp.concatenate([pack(tokens), meta], 1))
    got_dy = to_owner(pack(grad_out))
    n_own = got_x.shape[0]
    n_rows = RING * n_own
    half = n_rows // 2

    all_dy = lax.all_gather(got_dy, ("x", "y"), axis=0)
    pieces = [got_x] + [shift(got_x, "x", n) for n in (1, -1, 2)]
    part = sds((half, quarter), BF16)
    top, bot, meta_all = kernel(
        rows_body, (part, part, sds((n_rows, LANES), BF16)), *pieces, specs=[VMEM] * 4
    )
    left_t = shift(top, "y", 1)
    right_b = shift(bot, "y", -1)
    left_b = shift(bot, "y", 1)
    right_t = shift(top, "y", -1)
    far_t = shift(left_t, "y", 1)
    far_b = shift(right_b, "y", -1)

    near = sds((n_rows, quarter), BF16)
    g_far = sds((n_own // 2, width), BF16)
    g_near = sds((n_own, width), BF16)
    n_shards = 2 * RING * RING
    sem = pltpu.SemaphoreType.DMA
    *parts, gw, gates = kernel(
        expert_body,
        (near, near, near, part, part, g_near, g_near, g_near, g_far, g_far,
         sds((n_shards, n_rows), F32), sds((n_rows, LANES), F32)),
        at, top, bot, left_t, left_b, right_t, right_b, far_t, far_b, all_dy, meta_all,
        gate, up, down, router.T,
        specs=[SMEM] + [ANY] * 13 + [VMEM],
        out_specs=(ANY,) * 10 + (VMEM, VMEM),
        scratch=[
            pltpu.VMEM((RING, n_rows, quarter), BF16), pltpu.VMEM((RING, n_rows, quarter), BF16),
            pltpu.VMEM((RING, quarter, n_ff), BF16), pltpu.VMEM((RING, quarter, n_ff), BF16),
            pltpu.VMEM((RING, n_ff, quarter), BF16), pltpu.VMEM((n_rows, LANES), BF16),
            pltpu.VMEM((RING, 4 * N_EXP, quarter), BF16),
            pltpu.VMEM((n_rows, n_ff), BF16), pltpu.VMEM((n_rows, n_ff), BF16),
            pltpu.VMEM((n_rows, n_ff), BF16), pltpu.VMEM((n_rows, 4 * N_EXP), BF16),
            pltpu.VMEM((RING, n_rows, quarter), BF16), pltpu.VMEM((RING, n_rows, quarter), BF16),
            sem((RING * RING,)), sem((RING * RING,)), sem((RING,)), sem((RING,)), sem((RING,)),
            sem((RING,)), sem((5 + 5 * RING,)),
        ],
        limit=44,
    )

    gw_all = lax.all_to_all(
        gw.reshape(n_shards, 2, n_rows // 2), ("x", "zh", "y"), 0, 0, tiled=True
    )
    gw_exp = lax.all_to_all(
        kernel(exchange_body, sds((N_EXP, 2, n_rows // 2), F32), gw_all, specs=[VMEM]),
        EXP, 0, 0, tiled=True,
    ).reshape(N_EXP, n_rows)
    column = kernel(
        column_body, sds((n_own, quarter // 4), BF16), at, gw_exp, gates, top, bot,
        specs=[SMEM] + [VMEM] * 4, scratch=[pltpu.VMEM((n_rows, LANES), F32)],
    )

    out_terms = ring_reduce(*parts[:5], "y")
    grad_terms = ring_reduce(*parts[5:], "x")
    out_x = sum_rows(at, *out_terms)
    grad_got = lax.all_to_all(sum_lanes(*grad_terms), "y", 0, 0, tiled=True)
    out_got = [out_x[0]] + [shift(out_x[i], "x", OFFS[i]) for i in (1, 2, 3)]
    final = kernel(
        last_body, sds((n_own, 2 * quarter + quarter // 4), BF16), *out_got, grad_got, column,
        specs=[VMEM] * 6,
    )
    final = lax.all_to_all(final.reshape(2 * N_EXP, CAP, -1), ZAX, 0, 0, tiled=True)
    res = sds((rows, quarter), BF16)
    moe_out, grad_tokens, grad_router = kernel(
        combine_body, (res, res, sds((N_EXP, quarter), F32)),
        jnp.concatenate([pick_b, pick_b], 1), final.reshape(2 * SLOTS, -1), specs=[VMEM] * 2,
    )
    return (moe_out, grad_tokens, grad_router.T)


def solution(mesh):
    fine = Mesh(mesh.devices.reshape(4, 2, 4, 2, 4), ("x", "zh", "zl", "c", "y"))
    return jax.shard_map(
        on_device,
        mesh=fine,
        in_specs=(
            P(ALL, "y"),
            P(ALL, None),
            P(),
            P(EXP, None, ("x", "zh", "y")),
            P(EXP, None, ("x", "zh", "y")),
            P(EXP, ("x", "zh", "y"), None),
            P(ALL, "y"),
        ),
        out_specs=(P(ALL, "y"), P(ALL, "y"), P("y", None)),
        check_vma=False,
    )
```

```python
import jax
import jax.numpy as jnp
from jax import lax
from jax.experimental import pallas as pl
from jax.experimental.pallas import tpu as pltpu
from jax.sharding import Mesh
from jax.sharding import PartitionSpec as P

F32 = jnp.float32
BF16 = jnp.bfloat16
ZAX = ("zh", "zl", "c")
EXP = ("zl", "c")
ALL = ("x", "zh", "zl", "c")
RING = 4
OFFS = (0, -1, 1, 2)
N_EXP = 8
CAP = 4
SLOTS = N_EXP * CAP
LANES = 128


def dot(a, b):
    return jnp.dot(a, b, preferred_element_type=F32)


def dot_t(a, b):
    return lax.dot_general(a, b, (((1,), (1,)), ((), ())), preferred_element_type=F32)


def shift(a, axis, n):
    return lax.ppermute(a, axis, [(i, (i + n) % RING) for i in range(RING)])


def sds(shape, dtype):
    return jax.ShapeDtypeStruct(shape, dtype)


VMEM = pl.BlockSpec(memory_space=pltpu.VMEM)
SMEM = pl.BlockSpec(memory_space=pltpu.SMEM)
HBM = pl.BlockSpec(memory_space=pltpu.HBM)


def kernel(body, outs, *args, specs, out_specs=None, scratch=(), limit=16):
    return pl.pallas_call(
        body,
        out_shape=outs,
        in_specs=list(specs),
        out_specs=out_specs or jax.tree.map(lambda _: VMEM, outs),
        scratch_shapes=list(scratch),
        compiler_params=pltpu.CompilerParams(vmem_limit_bytes=limit << 20),
    )(*args)


def spot(at, off):
    return (at + (off + RING)) % RING


def split_body(got, x_out, dy_out):
    width = x_out.shape[1]
    x_out[...] = got[:, :width]
    dy = got[:, width:]
    for i in range(RING):
        dy_out[i] = dy


def rows_body(own, left, right, far, top_out, bot_out, meta_out):
    n, width = own.shape
    for i, r in enumerate((own, left, right, far)):
        s = slice((i % 2) * n, (i % 2 + 1) * n)
        (top_out, bot_out)[i // 2][s] = r[:, : width - LANES]
        meta_out[i * n : (i + 1) * n] = r[:, width - LANES :]


def lanes_body(parts, top_out, bot_out):
    width = parts.shape[2]
    for i in range(RING):
        (top_out, bot_out)[i // 2][:, (i % 2) * width : (i % 2 + 1) * width] = parts[i]


def expert_body(
    at, x0t, x0b, x1t, x1b, x2t, x2b, x3t, x3b, d0t, d0b, d1t, d1b, d2t, d2b, d3t, d3b,
    meta, gate, up, down, router,
    m0, m1, m2, m3t, m3b, g0, g1, g2, g3t, g3b,
    gw_out, gates_out,
    rp, hb, ggb, gub, tlb, pb, mo, go, so,
):
    x_at, y_at, e_at = at[0], at[1], at[2]
    half, quarter = x0t.shape
    n = d0t.shape[0]
    n_rows = 2 * half

    def quarter_at(i):
        return pl.ds(pl.multiple_of(spot(y_at, OFFS[i]) * quarter, quarter), quarter)

    for k in range(RING):
        r0 = router[:, k * quarter : (k + 1) * quarter]
        r1 = r0 - r0.astype(BF16).astype(F32)
        r2 = r1 - r1.astype(BF16).astype(F32)
        rp[k] = jnp.concatenate([r0, r1, r2, jnp.zeros_like(r0)], 0).astype(BF16)

    pre_gate = pre_up = logits3 = raw = None
    for i in range(RING):
        pair = ((x0t, x0b), (x1t, x1b), (x2t, x2b), (x3t, x3b))[i]
        a = jnp.concatenate([pair[0][...], pair[1][...]], 0)
        q = quarter_at(i)
        g, u, l = dot(a, gate[q]), dot(a, up[q]), dot_t(a, rp[spot(y_at, OFFS[i])])
        pre_gate = g if i == 0 else pre_gate + g
        pre_up = u if i == 0 else pre_up + u
        logits3 = l if i == 0 else logits3 + l
    for k in range(RING):
        group = ((d0t, d1t, d2t, d3t), (d0b, d1b, d2b, d3b))[k // 2]
        s = slice((k % 2) * quarter, (k % 2 + 1) * quarter)
        a = jnp.concatenate([d[:, s] for d in group], 0)
        g = dot_t(a, down[:, k * quarter : (k + 1) * quarter])
        raw = g if k == 0 else raw + g

    lane = lax.broadcasted_iota(jnp.int32, logits3.shape, 1)
    expert = lane % N_EXP
    code = meta[:, :1].astype(F32).astype(jnp.int32)
    other = code // CAP
    hot_own = expert == e_at
    hot_other = expert == other
    score_own = jax.nn.sigmoid(jnp.sum(jnp.where(hot_own, logits3, 0.0), 1, keepdims=True))
    score_other = jax.nn.sigmoid(jnp.sum(jnp.where(hot_other, logits3, 0.0), 1, keepdims=True))
    total = score_own + score_other
    weight = score_own / total
    both = score_own * score_other / (total * total)
    c_own = both * (1.0 - score_own)
    c_other = both * (1.0 - score_other)
    gate_sig = jax.nn.sigmoid(pre_gate)
    gate_act = pre_gate * gate_sig
    hidden = gate_act * pre_up
    product = hidden * raw
    grad_weight = jnp.sum(product, 1, keepdims=True)
    hb[...] = (weight * hidden).astype(BF16)
    grad_hidden = weight * raw
    ggb[...] = (
        grad_hidden * pre_up * gate_sig * (1.0 + pre_gate * (1.0 - gate_sig))
    ).astype(BF16)
    gub[...] = (grad_hidden * gate_act).astype(BF16)
    to_logits = jnp.where(hot_own, grad_weight * c_own, 0.0) - jnp.where(
        hot_other, grad_weight * c_other, 0.0
    )
    high = to_logits.astype(BF16).astype(F32)
    tlb[...] = jnp.where(lane < 2 * N_EXP, high, to_logits - high).astype(BF16)
    wide = lax.broadcasted_iota(jnp.int32, gates_out.shape, 1)
    gates_out[...] = jnp.where(wide == 0, c_own, code.astype(F32))
    for i in range(RING):
        row = pl.ds(pl.multiple_of(spot(x_at, OFFS[i]) * n, n), n)
        pb[row, :] = product[i * n : (i + 1) * n]
    ones = jnp.ones((8, product.shape[1]), F32)
    sums = lax.dot_general(
        ones, pb[...], (((1,), (1,)), ((), ())),
        preferred_element_type=F32, precision=lax.Precision.HIGHEST,
    )
    for k in range(2):
        w = gw_out.shape[2]
        piece = sums[:1, k * w : (k + 1) * w]
        gw_out[:, k, :] = jnp.broadcast_to(piece, (gw_out.shape[0], w))

    outs = []

    def send(src, dst):
        c = pltpu.make_async_copy(src, dst, so.at[len(outs)])
        c.start()
        outs.append(c)

    for i in (3, 1, 2, 0):
        mo[i] = dot(hb[...], down[:, quarter_at(i)]).astype(BF16)
        if i == 3:
            send(mo.at[i, :half], m3t)
            send(mo.at[i, half:], m3b)
        else:
            send(mo.at[i], (m0, m1, m2)[i])
    for k in range(RING):
        s = slice(k * quarter, (k + 1) * quarter)
        r4 = jnp.concatenate([rp[k][: 2 * N_EXP], rp[k][: 2 * N_EXP]], 0)
        v = dot_t(ggb[...], gate[s]) + dot_t(gub[...], up[s]) + dot(tlb[...], r4)
        t = slice((k % 2) * quarter, (k % 2 + 1) * quarter)
        go[k // 2, :, t] = v.astype(BF16)
        if k % 2:
            send(go.at[k // 2, 3 * n : 4 * n], (g3t, g3b)[k // 2])
            two = slice((k - 1) * quarter, (k + 1) * quarter)
            for i in (1, 2, 0):
                send(go.at[k // 2, i * n : (i + 1) * n], (g0, g1, g2)[i].at[:, two])
    for c in outs:
        c.wait()


def exchange_body(gw_all, out):
    out[...] = jnp.broadcast_to(jnp.sum(gw_all[...], 0, keepdims=True), out.shape)


def column_body(at, gw, gates, top, bot, out):
    x_at, zh_at, e_at = at[0], at[3], at[2]
    n_rows = gates.shape[0]
    n = n_rows // RING
    n_half = top.shape[1] // 2
    row = jnp.concatenate(
        [lax.broadcasted_iota(jnp.int32, (n, n_rows), 0) + spot(x_at, o) * n for o in OFFS], 0
    )
    col = lax.broadcasted_iota(jnp.int32, (n_rows, n_rows), 1)
    code = gates[:, 1:2].astype(jnp.int32)
    mate = (row // CAP) * CAP + code % CAP

    def fetch(mask):
        return lax.dot_general(
            mask.astype(F32), gw[...], (((1,), (1,)), ((), ())),
            preferred_element_type=F32, precision=lax.Precision.HIGHEST,
        )

    lane = lax.broadcasted_iota(jnp.int32, (n_rows, N_EXP), 1)
    diff = jnp.where(lane == e_at, fetch(row == col), 0.0) - jnp.where(
        lane == code // CAP, fetch(mate == col), 0.0
    )
    gl = gates[:, :1] * jnp.sum(diff, 1, keepdims=True)
    feat = pl.ds(pl.multiple_of(zh_at * n_half, n_half), n_half)
    acc = None
    for i in range(RING):
        a = (top, bot)[i // 2][(i % 2) * n : (i % 2 + 1) * n, feat].astype(F32)
        s = jnp.sum(a * gl[i * n : (i + 1) * n], 0, keepdims=True)
        acc = s if i == 0 else acc + s
    q = n_half // 2
    high = acc.astype(BF16).astype(F32)
    low = acc - high
    four = jnp.concatenate([high[:, :q], high[:, q:], low[:, :q], low[:, q:]], 0)
    block = jnp.concatenate([four, four], 0)
    for k in range(out.shape[0] // 16):
        out[k * 16 : (k + 1) * 16] = jnp.concatenate([block, block], 0).astype(BF16)


def add(a, b):
    return (a.astype(F32) + b.astype(F32)).astype(BF16)


def add_rows_body(right, up, left, down, right_out, left_out):
    half = up.shape[0]
    right_out[:half] = add(right[:half], up[...])
    right_out[half:] = right[half:]
    left_out[:half] = left[:half]
    left_out[half:] = add(left[half:], down[...])


def add_lanes_body(right, up, left, down, right_out, left_out):
    half = up.shape[1]
    right_out[:, :half] = add(right[:, :half], up[...])
    right_out[:, half:] = right[:, half:]
    left_out[:, :half] = left[:, :half]
    left_out[:, half:] = add(left[:, half:], down[...])


def ring_reduce(body, own, left, right, far_a, far_b, axis):
    up = shift(far_a, axis, 1)
    down = shift(far_b, axis, -1)
    like = sds(right.shape, BF16)
    right, left = kernel(body, (like, like), right, up, left, down, specs=[VMEM] * 4)
    return own, shift(right, axis, 1), shift(left, axis, -1)


def sum_rows_body(a, b, c, o0, o1, o2, o3):
    n = o0.shape[0]
    for i, o in enumerate((o0, o1, o2, o3)):
        s = slice(i * n, (i + 1) * n)
        o[...] = (a[s].astype(F32) + b[s].astype(F32) + c[s].astype(F32)).astype(BF16)


def sum_lanes_body(a, b, c, out):
    width = out.shape[2]
    for i in range(RING):
        s = slice(i * width, (i + 1) * width)
        out[i] = (a[:, s].astype(F32) + b[:, s].astype(F32) + c[:, s].astype(F32)).astype(BF16)


def last_body(a0, a1, a2, a3, g, column, out):
    width = a0.shape[1]
    total = a0[...].astype(F32) + a1[...].astype(F32) + (a2[...].astype(F32) + a3[...].astype(F32))
    out[:, :width] = total.astype(BF16)
    total = g[0].astype(F32) + g[1].astype(F32) + (g[2].astype(F32) + g[3].astype(F32))
    out[:, width : 2 * width] = total.astype(BF16)
    out[:, 2 * width :] = column[...]


def combine_body(pick, got, moe_out, gt_out, gr_out):
    width = moe_out.shape[1]
    two = pick[...]
    moe_out[...] = dot(two, got[:, :width]).astype(BF16)
    gt_out[...] = dot(two, got[:, width : 2 * width]).astype(BF16)
    tail = got[:, 2 * width :]
    q = tail.shape[1]
    n_got = got.shape[0]
    e = lax.broadcasted_iota(jnp.int32, (N_EXP, n_got), 0)
    r = lax.broadcasted_iota(jnp.int32, (N_EXP, n_got), 1)
    for zh in range(2):
        for c in range(2):
            base = (zh * N_EXP + e) * CAP + c
            high, low = ((r == base + k).astype(F32).astype(BF16) for k in (0, 2))
            parts = dot(high, tail) + dot(low, tail)
            gr_out[:, (zh * 2 + c) * q : (zh * 2 + c + 1) * q] = parts


def on_device(tokens, routes, router, gate_proj, up_proj, down_proj, grad_out):
    rows, quarter = tokens.shape
    at = jnp.stack(
        [lax.axis_index("x"), lax.axis_index("y"), lax.axis_index(EXP), lax.axis_index("zh")]
    ).astype(jnp.int32)
    gate, up, down = gate_proj[0], up_proj[0], down_proj[0]
    n_ff = gate.shape[1]

    at, routes = lax.optimization_barrier((at, routes))

    flat = routes.reshape(-1)
    ids = jnp.arange(flat.shape[0], dtype=jnp.int32)
    same = (flat[:, None] == flat[None, :]) & (ids[None, :] < ids[:, None])
    slot = jnp.sum(same.astype(jnp.int32), axis=1)
    code = (flat * CAP + slot).reshape(rows, 2)
    lanes = jnp.arange(SLOTS, dtype=jnp.int32)
    hot = (code[:, :, None] == lanes[None, None, :]).astype(F32)
    pick_b = jnp.sum(hot, axis=1).astype(BF16)
    meta = jnp.sum(hot * code[:, ::-1, None].astype(F32), axis=(0, 1))

    def pack(a):
        return lax.dot_general(
            pick_b, a, (((0,), (0,)), ((), ())), preferred_element_type=F32
        ).astype(BF16)

    meta = jnp.broadcast_to(meta[:, None], (SLOTS, LANES)).astype(BF16)
    packed = jnp.concatenate([pack(tokens), meta, pack(grad_out)], 1).reshape(N_EXP, CAP, -1)
    got = lax.all_to_all(jnp.concatenate([packed, packed], 0), ZAX, 0, 0, tiled=True)
    got = got.reshape(2 * SLOTS, -1)
    n_own = got.shape[0]
    n_rows = RING * n_own
    half = n_rows // 2
    got_x, got_dy = kernel(
        split_body,
        (sds((n_own, quarter + LANES), BF16), sds((RING, n_own, quarter), BF16)),
        got, specs=[VMEM],
    )

    got_dy = lax.all_to_all(got_dy, "y", 0, 0, tiled=True)
    pieces = [got_x] + [shift(got_x, "x", n) for n in (1, -1, 2)]
    part = sds((half, quarter), BF16)
    top, bot, meta_all = kernel(
        rows_body, (part, part, sds((n_rows, LANES), BF16)), *pieces, specs=[VMEM] * 4
    )
    g_part = sds((n_own, 2 * quarter), BF16)
    d_top, d_bot = kernel(lanes_body, (g_part, g_part), got_dy, specs=[VMEM])

    def ring_gather(a, b, axis):
        left_a = shift(a, axis, 1)
        right_b = shift(b, axis, -1)
        left_b = shift(b, axis, 1)
        right_a = shift(a, axis, -1)
        return a, b, left_a, left_b, right_a, right_b, shift(left_a, axis, 1), shift(right_b, axis, -1)

    full_x = ring_gather(top, bot, "y")
    full_dy = ring_gather(d_top, d_bot, "x")

    sem = pltpu.SemaphoreType.DMA
    n_shards = 2 * RING * RING
    near = sds((n_rows, quarter), BF16)
    g_near = sds((n_own, RING * quarter), BF16)
    *parts, gw, gates = kernel(
        expert_body,
        (near,) * 3 + (part,) * 2 + (g_near,) * 3 + (g_part,) * 2
        + (sds((n_shards, 2, n_rows // 2), F32), sds((n_rows, LANES), F32)),
        at, *full_x, *full_dy, meta_all, gate, up, down, router.T,
        specs=[SMEM] + [VMEM] * 21,
        out_specs=(HBM,) * 10 + (VMEM, VMEM),
        scratch=[
            pltpu.VMEM((RING, 4 * N_EXP, quarter), BF16),
            pltpu.VMEM((n_rows, n_ff), BF16), pltpu.VMEM((n_rows, n_ff), BF16),
            pltpu.VMEM((n_rows, n_ff), BF16), pltpu.VMEM((n_rows, 4 * N_EXP), BF16),
            pltpu.VMEM((n_rows, n_ff), F32),
            pltpu.VMEM((RING, n_rows, quarter), BF16), pltpu.VMEM((2, n_rows, 2 * quarter), BF16),
            sem((13,)),
        ],
        limit=26,
    )

    out_terms = ring_reduce(add_rows_body, *parts[:5], "y")
    grad_terms = ring_reduce(add_lanes_body, *parts[5:], "x")

    grad_y = kernel(
        sum_lanes_body, sds((RING, n_own, quarter), BF16), *grad_terms, specs=[VMEM] * 3
    )

    gw_all = lax.all_to_all(gw, ("x", "zh", "y"), 0, 0, tiled=True)
    gw_exp = lax.all_to_all(
        kernel(exchange_body, sds((N_EXP, 2, n_rows // 2), F32), gw_all, specs=[VMEM]),
        EXP, 0, 0, tiled=True,
    ).reshape(N_EXP, n_rows)
    column = kernel(
        column_body, sds((n_own, quarter // 4), BF16), at, gw_exp, gates, top, bot,
        specs=[SMEM] + [VMEM] * 4,
    )

    piece = sds((n_own, quarter), BF16)
    out_x = kernel(sum_rows_body, (piece,) * RING, *out_terms, specs=[VMEM] * 3)
    grad_got = lax.all_to_all(grad_y, "y", 0, 0, tiled=True)
    out_got = [out_x[0]] + [shift(out_x[i], "x", OFFS[i]) for i in (1, 2, 3)]
    final = kernel(
        last_body, sds((n_own, 2 * quarter + quarter // 4), BF16), *out_got, grad_got, column,
        specs=[VMEM] * 6,
    )
    final = lax.all_to_all(final.reshape(2 * N_EXP, CAP, -1), ZAX, 0, 0, tiled=True)
    res = sds((rows, quarter), BF16)
    moe_out, grad_tokens, grad_router = kernel(
        combine_body, (res, res, sds((N_EXP, quarter), F32)),
        jnp.concatenate([pick_b, pick_b], 1), final.reshape(2 * SLOTS, -1), specs=[VMEM] * 2,
    )
    return (moe_out, grad_tokens, grad_router.T)


def solution(mesh):
    fine = Mesh(mesh.devices.reshape(4, 2, 4, 2, 4), ("x", "zh", "zl", "c", "y"))
    return jax.shard_map(
        on_device,
        mesh=fine,
        in_specs=(
            P(ALL, "y"),
            P(ALL, None),
            P(),
            P(EXP, None, ("x", "zh", "y")),
            P(EXP, None, ("x", "zh", "y")),
            P(EXP, ("x", "zh", "y"), None),
            P(ALL, "y"),
        ),
        out_specs=(P(ALL, "y"), P(ALL, "y"), P("y", None)),
        check_vma=False,
    )
```

```python
import jax
import jax.numpy as jnp
from jax import lax
from jax.experimental import pallas as pl
from jax.experimental.pallas import tpu as pltpu
from jax.sharding import Mesh
from jax.sharding import PartitionSpec as P

F32 = jnp.float32
BF16 = jnp.bfloat16
ZAX = ("zh", "zl", "c")
EXP = ("zl", "c")
ALL = ("x", "zh", "zl", "c")
RING = 4
OFFS = (0, -1, 1, 2)
N_EXP = 8
CAP = 4
SLOTS = N_EXP * CAP
LANES = 128


def dot(a, b):
    return jnp.dot(a, b, preferred_element_type=F32)


def dot_t(a, b):
    return lax.dot_general(a, b, (((1,), (1,)), ((), ())), preferred_element_type=F32)


def shift(a, axis, n):
    return lax.ppermute(a, axis, [(i, (i + n) % RING) for i in range(RING)])


def sds(shape, dtype):
    return jax.ShapeDtypeStruct(shape, dtype)


VMEM = pl.BlockSpec(memory_space=pltpu.VMEM)
SMEM = pl.BlockSpec(memory_space=pltpu.SMEM)
HBM = pl.BlockSpec(memory_space=pltpu.HBM)


def kernel(body, outs, *args, specs, out_specs=None, scratch=(), limit=16):
    return pl.pallas_call(
        body,
        out_shape=outs,
        in_specs=list(specs),
        out_specs=out_specs or jax.tree.map(lambda _: VMEM, outs),
        scratch_shapes=list(scratch),
        compiler_params=pltpu.CompilerParams(vmem_limit_bytes=limit << 20),
    )(*args)


def spot(at, off):
    return (at + (off + RING)) % RING


def split_body(got, x_out, dy_out):
    width = x_out.shape[1]
    x_out[...] = got[:, :width]
    dy = got[:, width:]
    for i in range(RING):
        dy_out[i] = dy


def rows_body(own, left, right, far, top_out, bot_out, meta_out):
    n, width = own.shape
    for i, r in enumerate((own, left, right, far)):
        s = slice((i % 2) * n, (i % 2 + 1) * n)
        (top_out, bot_out)[i // 2][s] = r[:, : width - LANES]
        meta_out[i * n : (i + 1) * n] = r[:, width - LANES :]


def lanes_body(parts, top_out, bot_out):
    width = parts.shape[2]
    for i in range(RING):
        (top_out, bot_out)[i // 2][:, (i % 2) * width : (i % 2 + 1) * width] = parts[i]


def fetch_body(gate, up, down, gate_out, up_out, down_out, sems):
    pairs = ((gate, gate_out), (up, up_out), (down, down_out))
    copies = [pltpu.make_async_copy(a, b, sems.at[i]) for i, (a, b) in enumerate(pairs)]
    for c in copies:
        c.start()
    for c in copies:
        c.wait()


def expert_body(
    at, x0t, x0b, x1t, x1b, x2t, x2b, x3t, x3b, d0t, d0b, d1t, d1b, d2t, d2b, d3t, d3b,
    meta, gate, up, down, router,
    m0, m1, m2, m3t, m3b, g0, g1, g2, g3t, g3b,
    gw_out, gates_out,
    rp, hb, ggb, gub, tlb, pb, mo, go, so,
):
    x_at, y_at, e_at = at[0], at[1], at[2]
    half, quarter = x0t.shape
    n = d0t.shape[0]
    n_rows = 2 * half

    def quarter_at(i):
        return pl.ds(pl.multiple_of(spot(y_at, OFFS[i]) * quarter, quarter), quarter)

    for k in range(RING):
        r0 = router[:, k * quarter : (k + 1) * quarter]
        r1 = r0 - r0.astype(BF16).astype(F32)
        r2 = r1 - r1.astype(BF16).astype(F32)
        rp[k] = jnp.concatenate([r0, r1, r2, jnp.zeros_like(r0)], 0).astype(BF16)

    pre_gate = pre_up = logits3 = raw = None
    for i in range(RING):
        pair = ((x0t, x0b), (x1t, x1b), (x2t, x2b), (x3t, x3b))[i]
        a = jnp.concatenate([pair[0][...], pair[1][...]], 0)
        q = quarter_at(i)
        g, u, l = dot(a, gate[q]), dot(a, up[q]), dot_t(a, rp[spot(y_at, OFFS[i])])
        pre_gate = g if i == 0 else pre_gate + g
        pre_up = u if i == 0 else pre_up + u
        logits3 = l if i == 0 else logits3 + l
    for k in range(RING):
        group = ((d0t, d1t, d2t, d3t), (d0b, d1b, d2b, d3b))[k // 2]
        s = slice((k % 2) * quarter, (k % 2 + 1) * quarter)
        a = jnp.concatenate([d[:, s] for d in group], 0)
        g = dot_t(a, down[:, k * quarter : (k + 1) * quarter])
        raw = g if k == 0 else raw + g

    lane = lax.broadcasted_iota(jnp.int32, logits3.shape, 1)
    expert = lane % N_EXP
    code = meta[:, :1].astype(F32).astype(jnp.int32)
    other = code // CAP
    hot_own = expert == e_at
    hot_other = expert == other
    score_own = jax.nn.sigmoid(jnp.sum(jnp.where(hot_own, logits3, 0.0), 1, keepdims=True))
    score_other = jax.nn.sigmoid(jnp.sum(jnp.where(hot_other, logits3, 0.0), 1, keepdims=True))
    total = score_own + score_other
    weight = score_own / total
    both = score_own * score_other / (total * total)
    c_own = both * (1.0 - score_own)
    c_other = both * (1.0 - score_other)
    gate_sig = jax.nn.sigmoid(pre_gate)
    gate_act = pre_gate * gate_sig
    hidden = gate_act * pre_up
    product = hidden * raw
    grad_weight = jnp.sum(product, 1, keepdims=True)
    hb[...] = (weight * hidden).astype(BF16)
    grad_hidden = weight * raw
    ggb[...] = (
        grad_hidden * pre_up * gate_sig * (1.0 + pre_gate * (1.0 - gate_sig))
    ).astype(BF16)
    gub[...] = (grad_hidden * gate_act).astype(BF16)
    to_logits = jnp.where(hot_own, grad_weight * c_own, 0.0) - jnp.where(
        hot_other, grad_weight * c_other, 0.0
    )
    high = to_logits.astype(BF16).astype(F32)
    tlb[...] = jnp.where(lane < 2 * N_EXP, high, to_logits - high).astype(BF16)
    wide = lax.broadcasted_iota(jnp.int32, gates_out.shape, 1)
    gates_out[...] = jnp.where(wide == 0, c_own, code.astype(F32))
    for i in range(RING):
        row = pl.ds(pl.multiple_of(spot(x_at, OFFS[i]) * n, n), n)
        pb[row, :] = product[i * n : (i + 1) * n]
    ones = jnp.ones((8, product.shape[1]), F32)
    sums = lax.dot_general(
        ones, pb[...], (((1,), (1,)), ((), ())),
        preferred_element_type=F32, precision=lax.Precision.HIGHEST,
    )
    for k in range(2):
        w = gw_out.shape[2]
        piece = sums[:1, k * w : (k + 1) * w]
        gw_out[:, k, :] = jnp.broadcast_to(piece, (gw_out.shape[0], w))

    outs = []

    def send(src, dst):
        c = pltpu.make_async_copy(src, dst, so.at[len(outs)])
        c.start()
        outs.append(c)

    for i in (3, 1, 2, 0):
        mo[i] = dot(hb[...], down[:, quarter_at(i)]).astype(BF16)
        if i == 3:
            send(mo.at[i, :half], m3t)
            send(mo.at[i, half:], m3b)
        else:
            send(mo.at[i], (m0, m1, m2)[i])
    for k in range(RING):
        s = slice(k * quarter, (k + 1) * quarter)
        r4 = jnp.concatenate([rp[k][: 2 * N_EXP], rp[k][: 2 * N_EXP]], 0)
        v = dot_t(ggb[...], gate[s]) + dot_t(gub[...], up[s]) + dot(tlb[...], r4)
        t = slice((k % 2) * quarter, (k % 2 + 1) * quarter)
        go[k // 2, :, t] = v.astype(BF16)
        if k % 2:
            send(go.at[k // 2, 3 * n : 4 * n], (g3t, g3b)[k // 2])
            two = slice((k - 1) * quarter, (k + 1) * quarter)
            for i in (1, 2, 0):
                send(go.at[k // 2, i * n : (i + 1) * n], (g0, g1, g2)[i].at[:, two])
    for c in outs:
        c.wait()


def exchange_body(gw_all, out):
    out[...] = jnp.broadcast_to(jnp.sum(gw_all[...], 0, keepdims=True), out.shape)


def column_body(at, gw, gates, top, bot, out):
    x_at, zh_at, e_at = at[0], at[3], at[2]
    n_rows = gates.shape[0]
    n = n_rows // RING
    n_half = top.shape[1] // 2
    row = jnp.concatenate(
        [lax.broadcasted_iota(jnp.int32, (n, n_rows), 0) + spot(x_at, o) * n for o in OFFS], 0
    )
    col = lax.broadcasted_iota(jnp.int32, (n_rows, n_rows), 1)
    code = gates[:, 1:2].astype(jnp.int32)
    mate = (row // CAP) * CAP + code % CAP

    def fetch(mask):
        return lax.dot_general(
            mask.astype(F32), gw[...], (((1,), (1,)), ((), ())),
            preferred_element_type=F32, precision=lax.Precision.HIGHEST,
        )

    lane = lax.broadcasted_iota(jnp.int32, (n_rows, N_EXP), 1)
    diff = jnp.where(lane == e_at, fetch(row == col), 0.0) - jnp.where(
        lane == code // CAP, fetch(mate == col), 0.0
    )
    gl = gates[:, :1] * jnp.sum(diff, 1, keepdims=True)
    feat = pl.ds(pl.multiple_of(zh_at * n_half, n_half), n_half)
    acc = None
    for i in range(RING):
        a = (top, bot)[i // 2][(i % 2) * n : (i % 2 + 1) * n, feat].astype(F32)
        s = jnp.sum(a * gl[i * n : (i + 1) * n], 0, keepdims=True)
        acc = s if i == 0 else acc + s
    q = n_half // 2
    high = acc.astype(BF16).astype(F32)
    low = acc - high
    four = jnp.concatenate([high[:, :q], high[:, q:], low[:, :q], low[:, q:]], 0)
    block = jnp.concatenate([four, four], 0)
    for k in range(out.shape[0] // 16):
        out[k * 16 : (k + 1) * 16] = jnp.concatenate([block, block], 0).astype(BF16)


def add(a, b):
    return (a.astype(F32) + b.astype(F32)).astype(BF16)


def add_rows_body(right, up, left, down, right_out, left_out):
    half = up.shape[0]
    right_out[:half] = add(right[:half], up[...])
    right_out[half:] = right[half:]
    left_out[:half] = left[:half]
    left_out[half:] = add(left[half:], down[...])


def add_lanes_body(right, up, left, down, right_out, left_out):
    half = up.shape[1]
    right_out[:, :half] = add(right[:, :half], up[...])
    right_out[:, half:] = right[:, half:]
    left_out[:, :half] = left[:, :half]
    left_out[:, half:] = add(left[:, half:], down[...])


def ring_reduce(body, own, left, right, far_a, far_b, axis):
    up = shift(far_a, axis, 1)
    down = shift(far_b, axis, -1)
    like = sds(right.shape, BF16)
    right, left = kernel(body, (like, like), right, up, left, down, specs=[VMEM] * 4)
    return own, shift(right, axis, 1), shift(left, axis, -1)


def sum_rows_body(a, b, c, o0, o1, o2, o3):
    n = o0.shape[0]
    for i, o in enumerate((o0, o1, o2, o3)):
        s = slice(i * n, (i + 1) * n)
        o[...] = (a[s].astype(F32) + b[s].astype(F32) + c[s].astype(F32)).astype(BF16)


def sum_lanes_body(a, b, c, out):
    width = out.shape[2]
    for i in range(RING):
        s = slice(i * width, (i + 1) * width)
        out[i] = (a[:, s].astype(F32) + b[:, s].astype(F32) + c[:, s].astype(F32)).astype(BF16)


def last_body(a0, a1, a2, a3, g, column, out):
    width = a0.shape[1]
    total = a0[...].astype(F32) + a1[...].astype(F32) + (a2[...].astype(F32) + a3[...].astype(F32))
    out[:, :width] = total.astype(BF16)
    total = g[0].astype(F32) + g[1].astype(F32) + (g[2].astype(F32) + g[3].astype(F32))
    out[:, width : 2 * width] = total.astype(BF16)
    out[:, 2 * width :] = column[...]


def combine_body(pick, got, moe_out, gt_out, gr_out):
    width = moe_out.shape[1]
    two = pick[...]
    moe_out[...] = dot(two, got[:, :width]).astype(BF16)
    gt_out[...] = dot(two, got[:, width : 2 * width]).astype(BF16)
    tail = got[:, 2 * width :]
    q = tail.shape[1]
    n_got = got.shape[0]
    e = lax.broadcasted_iota(jnp.int32, (N_EXP, n_got), 0)
    r = lax.broadcasted_iota(jnp.int32, (N_EXP, n_got), 1)
    for zh in range(2):
        for c in range(2):
            base = (zh * N_EXP + e) * CAP + c
            high, low = ((r == base + k).astype(F32).astype(BF16) for k in (0, 2))
            parts = dot(high, tail) + dot(low, tail)
            gr_out[:, (zh * 2 + c) * q : (zh * 2 + c + 1) * q] = parts


def on_device(tokens, routes, router, gate_proj, up_proj, down_proj, grad_out):
    rows, quarter = tokens.shape
    at = jnp.stack(
        [lax.axis_index("x"), lax.axis_index("y"), lax.axis_index(EXP), lax.axis_index("zh")]
    ).astype(jnp.int32)
    gate, up, down = gate_proj[0], up_proj[0], down_proj[0]
    n_ff = gate.shape[1]

    at, routes = lax.optimization_barrier((at, routes))

    flat = routes.reshape(-1)
    ids = jnp.arange(flat.shape[0], dtype=jnp.int32)
    same = (flat[:, None] == flat[None, :]) & (ids[None, :] < ids[:, None])
    slot = jnp.sum(same.astype(jnp.int32), axis=1)
    code = (flat * CAP + slot).reshape(rows, 2)
    lanes = jnp.arange(SLOTS, dtype=jnp.int32)
    hot = (code[:, :, None] == lanes[None, None, :]).astype(F32)
    pick_b = jnp.sum(hot, axis=1).astype(BF16)
    meta = jnp.sum(hot * code[:, ::-1, None].astype(F32), axis=(0, 1))

    def pack(a):
        return lax.dot_general(
            pick_b, a, (((0,), (0,)), ((), ())), preferred_element_type=F32
        ).astype(BF16)

    meta = jnp.broadcast_to(meta[:, None], (SLOTS, LANES)).astype(BF16)
    packed = jnp.concatenate([pack(tokens), meta, pack(grad_out)], 1).reshape(N_EXP, CAP, -1)
    got = lax.all_to_all(jnp.concatenate([packed, packed], 0), ZAX, 0, 0, tiled=True)
    got = got.reshape(2 * SLOTS, -1)
    n_own = got.shape[0]
    n_rows = RING * n_own
    half = n_rows // 2
    got_x, got_dy = kernel(
        split_body,
        (sds((n_own, quarter + LANES), BF16), sds((RING, n_own, quarter), BF16)),
        got, specs=[VMEM],
    )

    got_dy = lax.all_to_all(got_dy, "y", 0, 0, tiled=True)
    pieces = [got_x] + [shift(got_x, "x", n) for n in (1, -1, 2)]
    part = sds((half, quarter), BF16)
    top, bot, meta_all = kernel(
        rows_body, (part, part, sds((n_rows, LANES), BF16)), *pieces, specs=[VMEM] * 4
    )
    g_part = sds((n_own, 2 * quarter), BF16)
    d_top, d_bot = kernel(lanes_body, (g_part, g_part), got_dy, specs=[VMEM])

    def ring_gather(a, b, axis):
        left_a = shift(a, axis, 1)
        right_b = shift(b, axis, -1)
        left_b = shift(b, axis, 1)
        right_a = shift(a, axis, -1)
        return a, b, left_a, left_b, right_a, right_b, shift(left_a, axis, 1), shift(right_b, axis, -1)

    full_x = ring_gather(top, bot, "y")
    full_dy = ring_gather(d_top, d_bot, "x")

    sem = pltpu.SemaphoreType.DMA
    gate, up, down, _ = lax.optimization_barrier((gate, up, down, d_top))
    gate, up, down = kernel(
        fetch_body, tuple(sds(w.shape, BF16) for w in (gate, up, down)), gate, up, down,
        specs=[HBM] * 3, scratch=[sem((3,))], limit=1,
    )
    n_shards = 2 * RING * RING
    near = sds((n_rows, quarter), BF16)
    g_near = sds((n_own, RING * quarter), BF16)
    *parts, gw, gates = kernel(
        expert_body,
        (near,) * 3 + (part,) * 2 + (g_near,) * 3 + (g_part,) * 2
        + (sds((n_shards, 2, n_rows // 2), F32), sds((n_rows, LANES), F32)),
        at, *full_x, *full_dy, meta_all, gate, up, down, router.T,
        specs=[SMEM] + [VMEM] * 21,
        out_specs=(HBM,) * 10 + (VMEM, VMEM),
        scratch=[
            pltpu.VMEM((RING, 4 * N_EXP, quarter), BF16),
            pltpu.VMEM((n_rows, n_ff), BF16), pltpu.VMEM((n_rows, n_ff), BF16),
            pltpu.VMEM((n_rows, n_ff), BF16), pltpu.VMEM((n_rows, 4 * N_EXP), BF16),
            pltpu.VMEM((n_rows, n_ff), F32),
            pltpu.VMEM((RING, n_rows, quarter), BF16), pltpu.VMEM((2, n_rows, 2 * quarter), BF16),
            sem((13,)),
        ],
        limit=26,
    )

    out_terms = ring_reduce(add_rows_body, *parts[:5], "y")
    grad_terms = ring_reduce(add_lanes_body, *parts[5:], "x")

    grad_y = kernel(
        sum_lanes_body, sds((RING, n_own, quarter), BF16), *grad_terms, specs=[VMEM] * 3
    )

    gw_all = lax.all_to_all(gw, ("x", "zh", "y"), 0, 0, tiled=True)
    gw_exp = lax.all_to_all(
        kernel(exchange_body, sds((N_EXP, 2, n_rows // 2), F32), gw_all, specs=[VMEM]),
        EXP, 0, 0, tiled=True,
    ).reshape(N_EXP, n_rows)
    column = kernel(
        column_body, sds((n_own, quarter // 4), BF16), at, gw_exp, gates, top, bot,
        specs=[SMEM] + [VMEM] * 4,
    )

    piece = sds((n_own, quarter), BF16)
    out_x = kernel(sum_rows_body, (piece,) * RING, *out_terms, specs=[VMEM] * 3)
    grad_got = lax.all_to_all(grad_y, "y", 0, 0, tiled=True)
    out_got = [out_x[0]] + [shift(out_x[i], "x", OFFS[i]) for i in (1, 2, 3)]
    final = kernel(
        last_body, sds((n_own, 2 * quarter + quarter // 4), BF16), *out_got, grad_got, column,
        specs=[VMEM] * 6,
    )
    final = lax.all_to_all(final.reshape(2 * N_EXP, CAP, -1), ZAX, 0, 0, tiled=True)
    res = sds((rows, quarter), BF16)
    moe_out, grad_tokens, grad_router = kernel(
        combine_body, (res, res, sds((N_EXP, quarter), F32)),
        jnp.concatenate([pick_b, pick_b], 1), final.reshape(2 * SLOTS, -1), specs=[VMEM] * 2,
    )
    return (moe_out, grad_tokens, grad_router.T)


def solution(mesh):
    fine = Mesh(mesh.devices.reshape(4, 2, 4, 2, 4), ("x", "zh", "zl", "c", "y"))
    return jax.shard_map(
        on_device,
        mesh=fine,
        in_specs=(
            P(ALL, "y"),
            P(ALL, None),
            P(),
            P(EXP, None, ("x", "zh", "y")),
            P(EXP, None, ("x", "zh", "y")),
            P(EXP, ("x", "zh", "y"), None),
            P(ALL, "y"),
        ),
        out_specs=(P(ALL, "y"), P(ALL, "y"), P("y", None)),
        check_vma=False,
    )
```
